128 devices in a mesh: ctx: 16 (over z, y), tp: 8 (over x, core).
Axes of the slice: x: 4, y: 4, z: 4, core: 2. Of those that a mesh axis runs over, the one named last changes fastest.
Arguments:
- q_in: bfloat16 [8192, 8192], P('ctx', 'tp'), may hold values from -600 to 600
- k_in: bfloat16 [8192, 8192], P('ctx', 'tp'), may hold values from -6 to 6
- v_in: bfloat16 [8192, 8192], P('ctx', 'tp'), may hold values from -6 to 6
- short_weight: float32 [3, 7, 8192], P(None, None, 'tp'), may hold values from -2 to 2
- decay_rate: float32 [64, 16], P('tp'), may hold values from 2.4414063e-05 to 0.0333333333
- residue: float32 [64, 16], P('tp'), may hold values from -2 to 2
- skip: float32 [8192], P('tp'), may hold values from -6 to 6
- gain: float32 [8192], P('tp'), may hold values from 0.25 to 1.75
- d_out: bfloat16 [8192, 8192], P('ctx', 'tp'), may hold values from -12 to 12
Outputs:
- mixed: bfloat16 [8192, 8192], P('ctx', 'tp')
- grad_q: bfloat16 [8192, 8192], P('ctx', 'tp')
- grad_k: bfloat16 [8192, 8192], P('ctx', 'tp')
- grad_v: bfloat16 [8192, 8192], P('ctx', 'tp')
The draws below stay inside these ranges and needn't reach their ends.
All inputs are finite; a program needn't handle non-finite values.
Results may differ from the reference program's by a relative error of at most 0.0049.
Values may be sent and summed in bfloat16 or wider, within the bound.
A program may use at most 128 MiB of HBM per device.

```python
import math
import jax
import jax.numpy as jnp
from jax import lax

D = 8192
G = 64
GROUP_CH = 128
MODES = 16
KER = 7
BLK = 256
SEQ = 8192


def draw_q_in(key, part):
    key_noise, key_row, key_col = jax.random.split(key, 3)
    noise = jax.random.truncated_normal(key_noise, -4.0, 4.0, (SEQ, D), jnp.float32)
    row_scale = jnp.exp(jax.random.uniform(key_row, (SEQ, 1), jnp.float32, 0.0, math.log(10.0)))
    channel_pos = jnp.arange(D).astype(jnp.float32) / D
    col_scale = jnp.exp(math.log(10.0) * channel_pos + jax.random.uniform(key_col, (D,), jnp.float32, -0.35, 0.35))
    return (noise * row_scale * col_scale[None, :]).astype(jnp.bfloat16)


def draw_decay_rate(key, part):
    key_pick, key_slow, key_fast = jax.random.split(key, 3)
    slow_share = 0.5
    slow_pick = jax.random.uniform(key_pick, (G, MODES), jnp.float32) < slow_share
    slow_log = jax.random.uniform(key_slow, (G, MODES), jnp.float32, math.log(0.2 / SEQ), math.log(2.0 / SEQ))
    fast_log = jax.random.uniform(key_fast, (G, MODES), jnp.float32, math.log(2.0 / SEQ), math.log(1.0 / 30))
    return jnp.exp(jnp.where(slow_pick, slow_log, fast_log)).astype(jnp.float32)


def shard_levels(own_key, dims, cuts, least, top_value):
    def one(dim, shards_of):
        steps = jax.random.uniform(jax.random.fold_in(jax.random.fold_in(own_key, 6), dim), (shards_of,), jnp.float32, least / len(cuts), top_value / len(cuts))
        return jnp.repeat(jnp.exp(steps), dims[dim] // shards_of).reshape((-1,) + (1,) * (len(dims) - dim - 1))

    level = one(*cuts[0])
    for cut in cuts[1:]:
        level = level * one(*cut)
    return level


def gaussian(key, dims, scale, reach, cuts=(), held_as=jnp.bfloat16):
    entries = jax.random.normal(key, dims, jnp.float32) * scale
    if len(cuts) > 0:
        entries = shard_levels(key, dims, cuts, -0.22, 0.18) * entries
    return jnp.clip(entries, min=-reach, max=reach).astype(held_as)


def setup_inputs(seed: int = 0) -> dict:
    key_list = jax.random.split(jax.random.key(seed), 10)
    return {
        "q_in": draw_q_in(jax.random.fold_in(key_list[9], 71), 0),
        "k_in": gaussian(key_list[1], (SEQ, D), 1.0, 6.0, ((0, 16), (1, 8))),
        "v_in": gaussian(key_list[2], (SEQ, D), 1.0, 6.0, ((0, 16), (1, 8))),
        "short_weight": gaussian(key_list[3], (3, KER, D), KER ** -0.5, 2.0, ((2, 8),), jnp.float32),
        "decay_rate": draw_decay_rate(jax.random.fold_in(key_list[9], 71), 0),
        "residue": gaussian(key_list[5], (G, MODES), 0.35, 2.0, ((0, 8),), jnp.float32),
        "skip": gaussian(key_list[6], (D,), 1.0, 6.0, ((0, 8),), jnp.float32),
        "gain": jnp.clip(1.0 + 0.15 * jax.random.normal(key_list[7], (D,), jnp.float32), 0.25, 1.75),
        "d_out": gaussian(key_list[8], (SEQ, D), 2.0, 12.0, ((0, 16), (1, 8))),
    }


PRECISE = lax.Precision.HIGHEST
EPSILON = 1e-05

def filter_table(decay_rate, residue):
    return residue * jnp.sqrt(-jnp.expm1(-2.0 * decay_rate))

def toeplitz_tile(rate_table, coef_table):
    offset = jnp.arange(BLK)[:, None] - jnp.arange(BLK)[None, :]
    lag_matrix = jnp.maximum(offset, 0).astype(jnp.float32)
    mode_count = rate_table.shape[1]
    summed = coef_table[:, 0, None, None] * jnp.exp(-rate_table[:, 0, None, None] * lag_matrix[None])
    for mode_index in range(1, mode_count):
        summed = summed + coef_table[:, mode_index, None, None] * jnp.exp(-rate_table[:, mode_index, None, None] * lag_matrix[None])
    return jnp.where(offset[None] >= 0, summed, 0.0)

def block_terms(signal, rate_table, coef_table):
    row_count, groups, group_width = signal.shape
    blocks = row_count // BLK
    pieces = signal.reshape(blocks, BLK, groups, group_width)
    lag_values = jnp.arange(BLK).astype(jnp.float32)
    toeplitz = toeplitz_tile(rate_table, coef_table)
    within = jnp.einsum('gij,bjgc->bigc', toeplitz, pieces, precision=PRECISE)
    tail_decay = jnp.exp(-rate_table[:, :, None] * (BLK - 1 - lag_values))
    block_ends = jnp.einsum('gmj,bjgc->bgmc', tail_decay, pieces, precision=PRECISE)
    return (within, block_ends)

def finish(within, block_ends, rate_table, coef_table, entering):
    blocks, _, groups, group_width = within.shape
    positions = jnp.arange(blocks)
    block_gap = positions[:, None] - 1 - positions[None, :]
    spans = (BLK * jnp.maximum(block_gap, 0)).astype(jnp.float32)
    mixing = jnp.where(block_gap[None, None] >= 0, jnp.exp(-rate_table[:, :, None, None] * spans), 0.0)
    entry_decay = jnp.exp(-rate_table[None] * (BLK * positions).astype(jnp.float32)[:, None, None])
    starts = jnp.einsum('gmab,bgmc->agmc', mixing, block_ends, precision=PRECISE) + entry_decay[..., None] * entering[None]
    lag_values = jnp.arange(BLK).astype(jnp.float32)
    lead_decay = coef_table[:, :, None] * jnp.exp(-rate_table[:, :, None] * (lag_values + 1.0))
    across = jnp.einsum('gmi,bgmc->bigc', lead_decay, starts, precision=PRECISE)
    return (within + across).reshape(blocks * BLK, groups, group_width)

def long_conv(signal, rate_table, coef_table, entering):
    within, block_ends = block_terms(signal, rate_table, coef_table)
    return finish(within, block_ends, rate_table, coef_table, entering)

def causal_taps(extended, weights, length):
    summed = weights[0] * extended[KER - 1:KER - 1 + length]
    for tap_index in range(1, KER):
        summed = summed + weights[tap_index] * extended[KER - 1 - tap_index:KER - 1 - tap_index + length]
    return summed

def later_taps(extended, weights, length):
    summed = weights[0] * extended[0:length]
    for tap_index in range(1, KER):
        summed = summed + weights[tap_index] * extended[tap_index:tap_index + length]
    return summed

def causal_conv(signal, weights):
    length = signal.shape[0]
    padding = jnp.zeros((KER - 1, signal.shape[1]), jnp.float32)
    return causal_taps(jnp.concatenate([padding, signal], 0), weights, length)

def later_conv(signal, weights):
    length = signal.shape[0]
    padding = jnp.zeros((KER - 1, signal.shape[1]), jnp.float32)
    return later_taps(jnp.concatenate([signal, padding], 0), weights, length)

def by_group(array):
    return jnp.moveaxis(array.reshape(array.shape[0], G, GROUP_CH), 1, 0)

def from_group(array):
    return jnp.moveaxis(array, 0, 1).reshape(array.shape[1], G * GROUP_CH)

def reference(q_in, k_in, v_in, short_weight, decay_rate, residue, skip, gain, d_out):
    q_groups = by_group(q_in)
    k_groups = by_group(k_in)
    v_groups = by_group(v_in)
    w_groups = jnp.moveaxis(short_weight.reshape(3, KER, G, GROUP_CH), 2, 0)
    skip_groups = skip.reshape(G, GROUP_CH)
    gain_groups = gain.reshape(G, GROUP_CH)
    coef_table = filter_table(decay_rate, residue)
    empty_state = jnp.zeros((1, MODES, GROUP_CH), jnp.float32)

    def shorts(member):
        q_part, k_part, v_part, w_part = member
        q_short = causal_conv(q_part.astype(jnp.float32), w_part[0])
        k_short = causal_conv(k_part.astype(jnp.float32), w_part[1])
        v_short = causal_conv(v_part.astype(jnp.float32), w_part[2])
        return (q_short, k_short, v_short)

    def forward_group(member):
        q_part, k_part, v_part, w_part, rate_row, coef_row, skip_row = member
        q_short, k_short, v_short = shorts((q_part, k_part, v_part, w_part))
        product = (k_short * v_short).astype(jnp.bfloat16)
        wide = product.astype(jnp.float32)
        carried = long_conv(wide[:, None, :], rate_row[None], coef_row[None], empty_state)[:, 0, :]
        filtered = carried + skip_row * wide
        return (q_short * filtered, filtered)
    gated, filtered = lax.map(forward_group, (q_groups, k_groups, v_groups, w_groups, decay_rate, coef_table, skip_groups))
    d_scaled = by_group(d_out).astype(jnp.float32) * gain_groups[:, None, :]
    scale = lax.rsqrt(lax.optimization_barrier(jnp.sum(gated * gated, axis=(0, 2))) / D + EPSILON)
    cross_mean = lax.optimization_barrier(jnp.sum(d_scaled * gated, axis=(0, 2))) / D
    mixed = from_group((gated * scale[None, :, None] * gain_groups[:, None, :]).astype(jnp.bfloat16))
    d_gated = scale[None, :, None] * d_scaled - (scale ** 3 * cross_mean)[None, :, None] * gated

    def backward_group(member):
        q_part, k_part, v_part, w_part, rate_row, coef_row, skip_row, grad_part, filtered_part = member
        q_short, k_short, v_short = shorts((q_part, k_part, v_part, w_part))
        dq_short = grad_part * filtered_part
        d_filtered = (grad_part * q_short).astype(jnp.bfloat16)
        wide = d_filtered.astype(jnp.float32)
        carried_back = long_conv(wide[::-1][:, None, :], rate_row[None], coef_row[None], empty_state)[:, 0, :][::-1]
        d_product = carried_back + skip_row * wide
        dk_short = d_product * v_short
        dv_short = d_product * k_short
        grad_q = later_conv(dq_short, w_part[0]).astype(jnp.bfloat16)
        grad_k = later_conv(dk_short, w_part[1]).astype(jnp.bfloat16)
        grad_v = later_conv(dv_short, w_part[2]).astype(jnp.bfloat16)
        return (grad_q, grad_k, grad_v)
    grad_q, grad_k, grad_v = lax.map(backward_group, (q_groups, k_groups, v_groups, w_groups, decay_rate, coef_table, skip_groups, d_gated, filtered))
    return (mixed, from_group(grad_q), from_group(grad_k), from_group(grad_v))
```

```python
import functools

import jax
import jax.numpy as jnp
from jax import lax
from jax.experimental import pallas as pl
from jax.experimental.pallas import tpu as pltpu
from jax.sharding import PartitionSpec as P

KER = 7
MODES = 16
GROUP_CH = 128
EPSILON = 1e-05
NZ = 4
NY = 4
ROWS = 64
MESH = pl.DeviceIdType.MESH
F32 = jnp.float32
BF16 = jnp.bfloat16


def split(x):
    hi = x.astype(BF16)
    lo = (x - hi.astype(F32)).astype(BF16)
    return hi, lo


def mm(a, b):
    return jnp.dot(a, b, preferred_element_type=F32)


def kernel(
    ntp,
    q_hbm, k_hbm, v_hbm, d_hbm, w_hbm, rate_hbm, res_hbm, skip_hbm, gain_hbm,
    mixed_hbm, gq_hbm, gk_hbm, gv_hbm,
    xin, win, ratein, resin, skipin, gainin,
    halo, xs, qs, ks, vs, pb, fw, grads, outs,
    wf, wb, leadf, leadb, tailf, tailb, wts,
    acc, scales, xpart, sy, sz, cs,
    in_sem, par_sem, out_sem,
    hsend, hrecv, ysend, yrecv, zsend, zrecv, csend, crecv, gsend, grecv,
):
    groups = xin.shape[1]
    length = xin.shape[2]
    nctx = NZ * NY
    half = length // 2
    me = lax.axis_index("ctx")
    tp = lax.axis_index("tp")
    z = lax.div(me, NY)
    y = lax.rem(me, NY)
    behind = lax.rem(me + nctx - 1, nctx)
    ahead = lax.rem(me + 1, nctx)

    bar = pltpu.get_barrier_semaphore()

    def greet(c, t):
        pl.semaphore_signal(bar, inc=1, device_id=(c, t), device_id_type=MESH)

    def ypeer(step):
        return z * NY + lax.rem(y + step, NY)

    def zpeer(step):
        return lax.rem(z + step, NZ) * NY + y

    for step in range(1, NY):
        greet(ypeer(step), tp)
    for step in range(1, NZ):
        greet(zpeer(step), tp)
    greet(behind, tp)
    greet(ahead, tp)
    for step in range(1, ntp):
        greet(me, lax.rem(tp + step, ntp))

    params = [
        pltpu.make_async_copy(src, dst, par_sem.at[i])
        for i, (src, dst) in enumerate(
            ((rate_hbm, ratein), (res_hbm, resin), (w_hbm, win), (skip_hbm, skipin), (gain_hbm, gainin))
        )
    ]
    for copy in params:
        copy.start()

    def cols(g):
        return pl.ds(pl.multiple_of(g * GROUP_CH, GROUP_CH), GROUP_CH)

    def load(a, g):
        src = (q_hbm, k_hbm, v_hbm, d_hbm)[a]
        return pltpu.make_async_copy(src.at[:, cols(g)], xin.at[a, g], in_sem.at[a, g])

    for a in range(4):
        @pl.loop(0, groups)
        def _(g):
            load(a, g).start()

    for copy in params:
        copy.wait()

    states = groups * MODES
    rate = ratein[...]
    r2 = rate * rate
    sinhc = 1.0 + r2 * (1 / 6) * (1.0 + r2 * (1 / 20) * (1.0 + r2 * (1 / 42) * (1.0 + r2 * (1 / 72) * (1.0 + r2 * (1 / 110)))))
    coef = resin[...] * jnp.sqrt(2.0 * rate * jnp.exp(-rate) * sinhc)
    row_i = lax.broadcasted_iota(jnp.int32, (MODES, MODES), 0)
    col_i = lax.broadcasted_iota(jnp.int32, (MODES, MODES), 1)

    def column(x):
        parts = [
            jnp.sum(jnp.where(row_i == col_i, jnp.broadcast_to(x[g : g + 1, :], (MODES, MODES)), 0.0), axis=1, keepdims=True)
            for g in range(groups)
        ]
        return jnp.concatenate(parts, axis=0)

    rate_wide = jnp.broadcast_to(column(rate), (states, GROUP_CH))
    coef_wide = jnp.broadcast_to(column(coef), (states, GROUP_CH))
    rate_row = rate_wide.T[0:1, :]
    coef_row = coef_wide.T[0:1, :]

    lag = lax.broadcasted_iota(jnp.int32, (states, GROUP_CH), 1).astype(F32)
    for b in range(length // GROUP_CH):
        at = lag + float(b * GROUP_CH)
        fh, fl = split(jnp.exp(-rate_wide * (float(length - 1) - at)))
        bh, bl = split(jnp.exp(-rate_wide * at))
        c = slice(b * GROUP_CH, (b + 1) * GROUP_CH)
        for g in range(groups):
            m = slice(g * MODES, (g + 1) * MODES)
            tailf[g, 0:MODES, c] = fh[m]
            tailf[g, MODES : 2 * MODES, c] = fl[m]
            tailb[g, 0:MODES, c] = bh[m]
            tailb[g, MODES : 2 * MODES, c] = bl[m]

    t_idx = lax.broadcasted_iota(jnp.int32, (GROUP_CH, states), 0).astype(F32)
    for b in range(length // GROUP_CH):
        at = t_idx + float(b * GROUP_CH)
        r = slice(b * GROUP_CH, (b + 1) * GROUP_CH)
        for lead, expo in ((leadf, at + 1.0), (leadb, float(length) - at)):
            hi, lo = split(coef_row * jnp.exp(-rate_row * expo))
            lead[r, 0:states] = hi
            lead[r, states : 2 * states] = hi
            lead[r, 2 * states : 3 * states] = lo

    for i in range(4):
        fi = jnp.float32(i)
        yf = y.astype(F32)
        zf = z.astype(F32)
        span = rate_wide * float(length)

        def weight(count, live):
            return jnp.where(live, jnp.exp(-span * jnp.maximum(count, 0.0)), 0.0)

        wts[0, i] = weight(yf - 1.0 - fi, i < y)
        wts[1, i] = jnp.exp(-span * float(NY - 1 - i))
        wts[2, i] = weight(NY * (zf - 1.0 - fi) + yf, i < z)
        wts[3, i] = weight(fi - yf - 1.0, i > y)
        wts[4, i] = jnp.exp(-span * float(i))
        wts[5, i] = weight(NY * (fi - zf - 1.0) + (NY - 1.0 - yf), i > z)

    pl.semaphore_wait(bar, 2 + NY - 1 + NZ - 1 + ntp - 1)

    def halo_copy(a):
        src = (q_hbm, k_hbm, v_hbm)[a]
        return pltpu.make_async_remote_copy(
            src_ref=src.at[pl.ds(length - 8, 8), :],
            dst_ref=halo.at[a],
            send_sem=hsend.at[a],
            recv_sem=hrecv.at[a],
            device_id=(ahead, tp),
            device_id_type=MESH,
        )

    for a in (1, 2, 0):
        halo_copy(a).start()

    i_idx = lax.broadcasted_iota(jnp.int32, (half, states), 0)
    lane_group = lax.broadcasted_iota(jnp.int32, (half, states), 1) // MODES
    grow_b = coef_row * jnp.exp(rate_row * i_idx.astype(F32))
    grow_f = coef_row * jnp.exp(rate_row * (float(half - 1) - i_idx.astype(F32)))
    ti = lax.broadcasted_iota(jnp.int32, (half, half), 0)
    tj = lax.broadcasted_iota(jnp.int32, (half, half), 1)
    acc[0, 0:half, :] = grow_f
    acc[1, 0:half, :] = grow_b

    @pl.loop(0, groups)
    def _(g):
        for a, (table, tail) in enumerate(((wf, tailf), (wb, tailb))):
            grow = acc[a, 0:half, :]
            pick = jnp.where(
                lax.broadcasted_iota(jnp.int32, (states, MODES), 0) == g * MODES + lax.broadcasted_iota(jnp.int32, (states, MODES), 1),
                1.0, 0.0,
            ).astype(BF16)
            hi, lo = split(grow)
            hi = mm(hi, pick).astype(BF16)
            lo = mm(lo, pick).astype(BF16)
            for b in range(2):
                c = slice(b * half, (b + 1) * half)
                th = tail[g, 0:MODES, c]
                tl = tail[g, MODES : 2 * MODES, c]
                w = mm(hi, th) + mm(hi, tl) + mm(lo, th)
                if a == 0 and b == 1:
                    w = jnp.where(ti >= tj, w, 0.0)
                if a == 1 and b == 0:
                    w = jnp.where(tj >= ti, w, 0.0)
                table[g, :, c] = w.astype(BF16)

    inner = (me > 0).astype(F32)
    final = (me < nctx - 1).astype(F32)

    def taps(a, g):
        return [win[a, j : j + 1, cols(g)] for j in range(KER)]

    def causal(slot, w, lo, rows):
        total = w[0] * xs[slot, pl.ds(8 + lo, rows), :]
        for j in range(1, KER):
            total = total + w[j] * xs[slot, pl.ds(8 + lo - j, rows), :]
        return total

    def later(a, g, w, lo, rows):
        total = w[0] * grads[a, g, pl.ds(lo, rows), :]
        for j in range(1, KER):
            total = total + w[j] * grads[a, g, pl.ds(lo + j, rows), :]
        return total

    @pl.loop(0, groups)
    def _(g):
        load(0, g).wait()
        for lo in range(0, length, ROWS):
            xs[0, 8 + lo : 8 + lo + ROWS, :] = xin[0, g, lo : lo + ROWS, :].astype(F32)
        w = taps(0, g)
        qs[g, 8:ROWS, :] = causal(0, w, 8, ROWS - 8)
        for lo in range(ROWS, length, ROWS):
            qs[g, lo : lo + ROWS, :] = causal(0, w, lo, ROWS)

    for a in (1, 2, 0):
        halo_copy(a).wait_recv()

    def state_copy(buf, send, recv, mine, d, g, step, peer):
        return pltpu.make_async_remote_copy(
            src_ref=buf.at[d, mine, g],
            dst_ref=buf.at[d, mine, g],
            send_sem=send.at[d, step, g],
            recv_sem=recv.at[d, mine, g],
            device_id=(peer, tp),
            device_id_type=MESH,
        )

    def y_start(d, g):
        for step in (1, 3, 2):
            state_copy(sy, ysend, yrecv, y, d, g, step, ypeer(step)).start()

    def z_start(d, g):
        for step in (1, 3, 2):
            state_copy(sz, zsend, zrecv, z, d, g, step, zpeer(step)).start()

    def arrived(buf, recv, d, g, slot):
        pltpu.make_async_copy(buf.at[d, slot, g], buf.at[d, slot, g], recv.at[d, slot, g]).wait()

    def y_total(d, g):
        m = pl.ds(pl.multiple_of(g * MODES, MODES), MODES)
        for step in (1, 3, 2):
            arrived(sy, yrecv, d, g, lax.rem(y + step, NY))
        part = jnp.zeros((MODES, GROUP_CH), F32)
        total = jnp.zeros((MODES, GROUP_CH), F32)
        for i in range(NY):
            s = sy[d, i, g]
            part = part + wts[3 * d, i, m, :] * s
            total = total + wts[3 * d + 1, i, m, :] * s
        xpart[g] = part
        sz[d, z, g] = total
        z_start(d, g)

    zero_state = jnp.zeros((MODES, GROUP_CH), F32)
    state_row = lax.broadcasted_iota(jnp.int32, (states, GROUP_CH), 0) // MODES

    def entering(d, g):
        m = pl.ds(pl.multiple_of(g * MODES, MODES), MODES)
        for step in (1, 3, 2):
            arrived(sz, zrecv, d, g, lax.rem(z + step, NZ))
        x = xpart[g]
        for i in range(NZ):
            x = x + wts[3 * d + 2, i, m, :] * sz[d, i, g]
        full = jnp.where(state_row == g, jnp.concatenate([x] * groups, axis=0), 0.0)
        hi, lo = split(full)
        return jnp.concatenate([hi, lo, hi], axis=0)

    @pl.loop(0, groups)
    def _(g):
        load(1, g).wait()
        load(2, g).wait()
        for a in (0, 1, 2):
            xs[a, 0:8, :] = halo[a, :, cols(g)].astype(F32) * inner
        xs[0, 8:16, :] = xin[0, g, 0:16, :].astype(F32)[0:8]
        qs[g, 0:8, :] = causal(0, taps(0, g), 0, 8)
        for a in (1, 2):
            for lo in range(0, length, ROWS):
                xs[a, 8 + lo : 8 + lo + ROWS, :] = xin[a, g, lo : lo + ROWS, :].astype(F32)
        wk = taps(1, g)
        wv = taps(2, g)
        for lo in range(0, length, ROWS):
            kk = causal(1, wk, lo, ROWS)
            vv = causal(2, wv, lo, ROWS)
            ks[g, lo : lo + ROWS, :] = kk
            vs[g, lo : lo + ROWS, :] = vv
            pb[g, lo : lo + ROWS, :] = (kk * vv).astype(BF16)
        s = mm(tailf[g], pb[g])
        sy[0, y, g] = s[0:MODES] + s[MODES : 2 * MODES]
        y_start(0, g)

    @pl.loop(0, groups)
    def _(g):
        y_total(0, g)
        skip = skipin[pl.ds(g, 1), :]
        head = pb[g, 0:half, :]
        fw[g, 0:half, :] = mm(wf[g, :, half:length], head) + skip * head.astype(F32)
        fw[g, half:length, :] = mm(wf[g], pb[g]) + skip * pb[g, half:length, :].astype(F32)

    acc[...] = jnp.zeros_like(acc)

    @pl.loop(0, groups)
    def _(g):
        load(3, g).wait()
        state = entering(0, g)
        gain = gainin[pl.ds(g, 1), :]
        for lo in range(0, length, GROUP_CH):
            r = slice(lo, lo + GROUP_CH)
            f = fw[g, r, :] + mm(leadf[r, :], state)
            fw[g, r, :] = f
            gated = qs[g, r, :] * f
            acc[0, r, :] += gated * gated
            acc[1, r, :] += (xin[3, g, r, :].astype(F32) * gain) * gated

    sums = []
    for a in range(2):
        for lo in range(0, length, GROUP_CH):
            sums.append(jnp.sum(acc[a, lo : lo + GROUP_CH, :].T, axis=0, keepdims=True))
    cs[tp] = jnp.concatenate(sums, axis=0)

    def sums_copy(step):
        return pltpu.make_async_remote_copy(
            src_ref=cs.at[tp],
            dst_ref=cs.at[tp],
            send_sem=csend.at[step],
            recv_sem=crecv.at[tp],
            device_id=(me, lax.rem(tp + step, ntp)),
            device_id_type=MESH,
        )

    for step in range(1, ntp):
        sums_copy(step).start()
    for step in range(1, ntp):
        slot = lax.rem(tp + step, ntp)
        pltpu.make_async_copy(cs.at[slot], cs.at[slot], crecv.at[slot]).wait()
    total = cs[0]
    for i in range(1, ntp):
        total = total + cs[i]
    width = float(groups * GROUP_CH * ntp)
    blocks = length // GROUP_CH
    scale = lax.rsqrt(total[0:blocks] / width + EPSILON)
    cubed = scale * scale * scale * (total[blocks : 2 * blocks] / width)
    for b in range(blocks):
        r = slice(b * GROUP_CH, (b + 1) * GROUP_CH)
        scales[0, r, :] = jnp.broadcast_to(scale[b : b + 1, :], (GROUP_CH, GROUP_CH)).T
        scales[1, r, :] = jnp.broadcast_to(cubed[b : b + 1, :], (GROUP_CH, GROUP_CH)).T

    def edge_copy(a, g):
        return pltpu.make_async_remote_copy(
            src_ref=grads.at[a, g, pl.ds(0, 8), :],
            dst_ref=grads.at[a, g, pl.ds(length, 8), :],
            send_sem=gsend.at[a, g],
            recv_sem=grecv.at[a, g],
            device_id=(behind, tp),
            device_id_type=MESH,
        )

    def store(a, g):
        dst = (mixed_hbm, gq_hbm, gk_hbm, gv_hbm)[a]
        return pltpu.make_async_copy(outs.at[a, g], dst.at[:, cols(g)], out_sem.at[a, g])

    @pl.loop(0, groups)
    def _(g):
        gain = gainin[pl.ds(g, 1), :]
        for lo in range(0, length, ROWS):
            r = slice(lo, lo + ROWS)
            q = qs[g, r, :]
            f = fw[g, r, :]
            gated = q * f
            scale = scales[0, r, :]
            outs[0, g, r, :] = (gated * scale * gain).astype(BF16)
            d_gated = scale * (xin[3, g, r, :].astype(F32) * gain) - scales[1, r, :] * gated
            grads[0, g, r, :] = d_gated * f
            pb[g, r, :] = (d_gated * q).astype(BF16)
        s = mm(tailb[g], pb[g])
        sy[1, y, g] = s[0:MODES] + s[MODES : 2 * MODES]
        y_start(1, g)
        edge_copy(0, g).start()
        store(0, g).start()

    @pl.loop(0, groups)
    def _(g):
        y_total(1, g)
        skip = skipin[pl.ds(g, 1), :]
        rest = pb[g, half:length, :]
        fw[g, 0:half, :] = mm(wb[g], pb[g]) + skip * pb[g, 0:half, :].astype(F32)
        fw[g, half:length, :] = mm(wb[g, :, 0:half], rest) + skip * rest.astype(F32)

    def finish(a, g):
        edge_copy(a, g).wait_recv()
        grads[a, g, length : length + 8, :] = grads[a, g, length : length + 8, :] * final
        w = taps(a, g)
        for lo in range(0, length, ROWS):
            outs[a + 1, g, lo : lo + ROWS, :] = later(a, g, w, lo, ROWS).astype(BF16)
        store(a + 1, g).start()

    @pl.loop(0, groups)
    def _(g):
        finish(0, g)

    @pl.loop(0, groups)
    def _(g):
        state = entering(1, g)
        for lo in range(0, length, GROUP_CH):
            r = slice(lo, lo + GROUP_CH)
            dp = fw[g, r, :] + mm(leadb[r, :], state)
            grads[1, g, r, :] = dp * vs[g, r, :]
            grads[2, g, r, :] = dp * ks[g, r, :]
        edge_copy(1, g).start()
        edge_copy(2, g).start()

    @pl.loop(0, groups)
    def _(g):
        finish(1, g)
        finish(2, g)

    for a in range(3):
        halo_copy(a).wait_send()
    for step in range(1, ntp):
        sums_copy(step).wait_send()

    @pl.loop(0, groups)
    def _(g):
        for d in range(2):
            for step in range(1, NY):
                state_copy(sy, ysend, yrecv, y, d, g, step, ypeer(step)).wait_send()
            for step in range(1, NZ):
                state_copy(sz, zsend, zrecv, z, d, g, step, zpeer(step)).wait_send()
        for a in range(3):
            edge_copy(a, g).wait_send()
        for a in range(4):
            store(a, g).wait()


def body(q_in, k_in, v_in, short_weight, decay_rate, residue, skip, gain, d_out):
    length, channels = q_in.shape
    groups = channels // GROUP_CH
    ntp = lax.axis_size("tp")
    half = length // 2
    states = groups * MODES
    vmem = pltpu.VMEM
    dma = pltpu.SemaphoreType.DMA
    result = jax.ShapeDtypeStruct((length, channels), BF16)
    scratch = [
        vmem((4, groups, length, GROUP_CH), BF16),
        vmem(short_weight.shape, F32),
        vmem((groups, MODES), F32),
        vmem((groups, MODES), F32),
        vmem((groups, GROUP_CH), F32),
        vmem((groups, GROUP_CH), F32),
        vmem((3, 8, channels), BF16),
        vmem((3, length + 8, GROUP_CH), F32),
        vmem((groups, length, GROUP_CH), F32),
        vmem((groups, length, GROUP_CH), F32),
        vmem((groups, length, GROUP_CH), F32),
        vmem((groups, length, GROUP_CH), BF16),
        vmem((groups, length, GROUP_CH), F32),
        vmem((3, groups, length + 8, GROUP_CH), F32),
        vmem((4, groups, length, GROUP_CH), BF16),
        vmem((groups, half, length), BF16),
        vmem((groups, half, length), BF16),
        vmem((length, 3 * states), BF16),
        vmem((length, 3 * states), BF16),
        vmem((groups, 2 * MODES, length), BF16),
        vmem((groups, 2 * MODES, length), BF16),
        vmem((6, 4, states, GROUP_CH), F32),
        vmem((2, length, GROUP_CH), F32),
        vmem((2, length, GROUP_CH), F32),
        vmem((groups, MODES, GROUP_CH), F32),
        vmem((2, NY, groups, MODES, GROUP_CH), F32),
        vmem((2, NZ, groups, MODES, GROUP_CH), F32),
        vmem((ntp, 8, GROUP_CH), F32),
        dma((4, groups)),
        dma((5,)),
        dma((4, groups)),
        dma((3,)),
        dma((3,)),
        dma((2, NY, groups)),
        dma((2, NY, groups)),
        dma((2, NZ, groups)),
        dma((2, NZ, groups)),
        dma((ntp,)),
        dma((ntp,)),
        dma((3, groups)),
        dma((3, groups)),
    ]
    return pl.pallas_call(
        functools.partial(kernel, ntp),
        out_shape=(result,) * 4,
        in_specs=[pl.BlockSpec(memory_space=pl.ANY)] * 9,
        out_specs=(pl.BlockSpec(memory_space=pl.ANY),) * 4,
        scratch_shapes=scratch,
        compiler_params=pltpu.CompilerParams(
            collective_id=0, has_side_effects=True, vmem_limit_bytes=60 * 1024 * 1024
        ),
        name="hyena_block",
    )(
        q_in, k_in, v_in, d_out, short_weight, decay_rate, residue,
        skip.reshape(groups, GROUP_CH), gain.reshape(groups, GROUP_CH),
    )


def solution(mesh):
    in_specs = (
        P("ctx", "tp"),
        P("ctx", "tp"),
        P("ctx", "tp"),
        P(None, None, "tp"),
        P("tp", None),
        P("tp", None),
        P("tp"),
        P("tp"),
        P("ctx", "tp"),
    )
    out_specs = (P("ctx", "tp"), P("ctx", "tp"), P("ctx", "tp"), P("ctx", "tp"))
    return jax.shard_map(body, mesh=mesh, in_specs=in_specs, out_specs=out_specs, check_vma=False)
```

```python
import functools

import jax
import jax.numpy as jnp
from jax import lax
from jax.experimental import pallas as pl
from jax.experimental.pallas import tpu as pltpu
from jax.sharding import PartitionSpec as P

KER = 7
MODES = 16
GROUP_CH = 128
EPSILON = 1e-05
NZ = 4
NY = 4
ROWS = 64
PAIR = 2
GRANT = 61_760_000
MESH = pl.DeviceIdType.MESH
F32 = jnp.float32
BF16 = jnp.bfloat16


def split(x):
    hi = x.astype(BF16)
    lo = (x - hi.astype(F32)).astype(BF16)
    return hi, lo


def mm(a, b):
    return jnp.dot(a, b, preferred_element_type=F32)


def cols(g):
    return pl.ds(pl.multiple_of(g * GROUP_CH, GROUP_CH), GROUP_CH)


def later(src, g, w, lo, rows):
    total = w[0] * src[g, pl.ds(lo, rows), :]
    for j in range(1, KER):
        total = total + w[j] * src[g, pl.ds(lo + j, rows), :]
    return total


def main_kernel(
    ntp,
    q_hbm, k_hbm, v_hbm, d_hbm, w_hbm, rate_hbm, res_hbm, skip_hbm, gain_hbm,
    mixed, gq, gk, dv,
    xin, win, ratein, resin, skipin, gainin,
    halo, xs, qs, ks, vs, pb, fw, dq, dk, edge,
    wf, wb, af, ab, tailf, tailb, ratew, rate3, coef3, dec, far,
    acc, scales, xpart, sy, sz, cs,
    in_sem, par_sem,
    hsend, hrecv, ysend, yrecv, zsend, zrecv, csend, crecv, gsend, grecv,
):
    length = xin.shape[1]
    groups = xin.shape[2] // GROUP_CH
    pairs = groups // PAIR
    states = groups * MODES
    blocks = length // GROUP_CH
    nctx = NZ * NY
    me = lax.axis_index("ctx")
    tp = lax.axis_index("tp")
    z = lax.div(me, NY)
    y = lax.rem(me, NY)
    behind = lax.rem(me + nctx - 1, nctx)
    ahead = lax.rem(me + 1, nctx)

    params = [
        pltpu.make_async_copy(src, dst, par_sem.at[i])
        for i, (src, dst) in enumerate(
            ((rate_hbm, ratein), (res_hbm, resin), (w_hbm, win), (skip_hbm, skipin), (gain_hbm, gainin))
        )
    ]
    for copy in params:
        copy.start()

    def load(a):
        return pltpu.make_async_copy((q_hbm, k_hbm, v_hbm, d_hbm)[a], xin.at[a], in_sem.at[a])

    for a in (1, 2, 0, 3):
        load(a).start()

    bar = pltpu.get_barrier_semaphore()

    def greet(c, t):
        pl.semaphore_signal(bar, inc=1, device_id=(c, t), device_id_type=MESH)

    def ypeer(step):
        return z * NY + lax.rem(y + step, NY)

    def zpeer(step):
        return lax.rem(z + step, NZ) * NY + y

    greet(behind, tp)
    greet(ahead, tp)
    for step in range(1, NY):
        greet(ypeer(step), tp)
    for step in range(1, NZ):
        greet(zpeer(step), tp)
    for step in range(1, ntp):
        greet(me, lax.rem(tp + step, ntp))

    for copy in params:
        copy.wait()

    rate = ratein[...]
    r2 = rate * rate
    sinhc = 1.0 + r2 * (1 / 6) * (1.0 + r2 * (1 / 20) * (1.0 + r2 * (1 / 42) * (1.0 + r2 * (1 / 72) * (1.0 + r2 * (1 / 110)))))
    coef = resin[...] * jnp.sqrt(2.0 * rate * jnp.exp(-rate) * sinhc)
    rate3[...] = jnp.concatenate([rate] * 3, axis=1)
    coef3[...] = jnp.concatenate([coef] * 3, axis=1)
    row_i = lax.broadcasted_iota(jnp.int32, (MODES, MODES), 0)
    col_i = lax.broadcasted_iota(jnp.int32, (MODES, MODES), 1)
    yf = y.astype(F32)
    for g in range(groups):
        m = slice(g * MODES, (g + 1) * MODES)
        column = jnp.sum(
            jnp.where(row_i == col_i, jnp.broadcast_to(rate[g : g + 1, :], (MODES, MODES)), 0.0), axis=1, keepdims=True
        )
        wide = jnp.broadcast_to(column, (MODES, GROUP_CH))
        ratew[m, :] = wide
        for i in range(blocks):
            dec[i, m, :] = jnp.exp(wide * (-1.0 * GROUP_CH * (i + 1)))
        far[0, m, :] = jnp.exp(wide * (-float(length) * yf))
        far[1, m, :] = jnp.exp(wide * (-float(length) * (NY - 1.0 - yf)))
        far[2, m, :] = jnp.exp(wide * (-float(length) * NY))

    i_idx = lax.broadcasted_iota(jnp.int32, (GROUP_CH, 3 * MODES), 0).astype(F32)
    first = lax.broadcasted_iota(jnp.int32, (GROUP_CH, 3 * MODES), 1) < 2 * MODES
    lag = lax.broadcasted_iota(jnp.int32, (MODES, GROUP_CH), 1).astype(F32)
    ti = lax.broadcasted_iota(jnp.int32, (GROUP_CH, GROUP_CH), 0)
    tj = lax.broadcasted_iota(jnp.int32, (GROUP_CH, GROUP_CH), 1)

    @pl.loop(0, pairs)
    def _(p):
        for e in range(PAIR):
            g = p * PAIR + e
            r_row = rate3[pl.ds(g, 1), :]
            c_row = coef3[pl.ds(g, 1), :]
            for a, expo in ((af, float(GROUP_CH - 1) - i_idx), (ab, i_idx)):
                x = c_row * jnp.exp(r_row * expo)
                hi = x.astype(BF16).astype(F32)
                a[g] = jnp.where(first, hi, x - hi).astype(BF16)
            wide = ratew[pl.ds(pl.multiple_of(g * MODES, MODES), MODES), :]
            for b in range(blocks):
                at = lag + float(b * GROUP_CH)
                c = slice(b * GROUP_CH, (b + 1) * GROUP_CH)
                for tail, expo in ((tailf, float(length - 1) - at), (tailb, at)):
                    hi, lo = split(jnp.exp(-wide * expo))
                    tail[g, 0:MODES, c] = hi
                    tail[g, MODES : 2 * MODES, c] = lo
                    tail[g, 2 * MODES : 3 * MODES, c] = hi
        for e in range(PAIR):
            g = p * PAIR + e
            for b in range(blocks):
                c = slice(b * GROUP_CH, (b + 1) * GROUP_CH)
                w = mm(af[g], tailf[g, :, c])
                if b == blocks - 1:
                    w = jnp.where(ti >= tj, w, 0.0)
                w = w.astype(BF16)
                wf[g, :, c] = w
                w = mm(ab[g], tailb[g, :, c])
                if b == 0:
                    w = jnp.where(tj >= ti, w, 0.0)
                w = w.astype(BF16)
                wb[g, :, c] = w

    pl.semaphore_wait(bar, 2 + NY - 1 + NZ - 1 + ntp - 1)

    def halo_copy(a):
        src = (q_hbm, k_hbm, v_hbm)[a]
        return pltpu.make_async_remote_copy(
            src_ref=src.at[pl.ds(length - 8, 8), :],
            dst_ref=halo.at[a],
            send_sem=hsend.at[a],
            recv_sem=hrecv.at[a],
            device_id=(ahead, tp),
            device_id_type=MESH,
        )

    for a in (1, 2, 0):
        halo_copy(a).start()

    inner = (me > 0).astype(F32)
    final = (me < nctx - 1).astype(F32)

    def taps(a, g):
        return [win[a, j : j + 1, cols(g)] for j in range(KER)]

    def stage(slot, a, g):
        xs[slot, 0:8, :] = halo[a, :, cols(g)].astype(F32) * inner
        for lo in range(0, length, ROWS):
            xs[slot, 8 + lo : 8 + lo + ROWS, :] = xin[a, lo : lo + ROWS, cols(g)].astype(F32)

    def causal(slot, w, lo, rows):
        total = w[0] * xs[slot, pl.ds(8 + lo, rows), :]
        for j in range(1, KER):
            total = total + w[j] * xs[slot, pl.ds(8 + lo - j, rows), :]
        return total

    def state_copy(buf, send, recv, mine, d, p, step, peer):
        return pltpu.make_async_remote_copy(
            src_ref=buf.at[d, mine, p],
            dst_ref=buf.at[d, mine, p],
            send_sem=send.at[d, step, p],
            recv_sem=recv.at[d, mine, p],
            device_id=(peer, tp),
            device_id_type=MESH,
        )

    def y_start(d, p):
        for step in (1, 3, 2):
            state_copy(sy, ysend, yrecv, y, d, p, step, ypeer(step)).start()

    def z_start(d, p):
        for step in (1, 3, 2):
            state_copy(sz, zsend, zrecv, z, d, p, step, zpeer(step)).start()

    def arrived(buf, recv, d, p, slot):
        pltpu.make_async_copy(buf.at[d, slot, p], buf.at[d, slot, p], recv.at[d, slot, p]).wait()

    def modes(g):
        return pl.ds(pl.multiple_of(g * MODES, MODES), MODES)

    def y_total(d, p):
        for step in (1, 3, 2):
            arrived(sy, yrecv, d, p, lax.rem(y + step, NY))
        for e in range(PAIR):
            g = p * PAIR + e
            decay = dec[blocks - 1, modes(g), :]
            part = jnp.zeros((MODES, GROUP_CH), F32)
            total = jnp.zeros((MODES, GROUP_CH), F32)
            for i in range(NY) if d == 0 else reversed(range(NY)):
                s = sy[d, i, p, e]
                before = (i < y) if d == 0 else (i > y)
                part = jnp.where(before, decay * part + s, part)
                total = decay * total + s
            xpart[p, e] = part
            sz[d, z, p, e] = total
        z_start(d, p)

    def z_wait(d, p):
        for step in (1, 3, 2):
            arrived(sz, zrecv, d, p, lax.rem(z + step, NZ))

    def entering(d, p, e):
        m = modes(p * PAIR + e)
        decay = far[2, m, :]
        total = jnp.zeros((MODES, GROUP_CH), F32)
        for i in range(NZ) if d == 0 else reversed(range(NZ)):
            before = (i < z) if d == 0 else (i > z)
            total = jnp.where(before, decay * total + sz[d, i, p, e], total)
        x = xpart[p, e] + far[d, m, :] * total
        parts = []
        for b in range(blocks):
            hi, lo = split(x * dec[b if d == 0 else blocks - 1 - b, m, :])
            parts.append(jnp.concatenate([hi, lo, hi], axis=0))
        return parts

    for a in (1, 2, 0):
        halo_copy(a).wait_recv()
    for a in range(3):
        load(a).wait()

    @pl.loop(0, pairs)
    def _(p):
        for e in range(PAIR):
            g = p * PAIR + e
            stage(2 * e, 1, g)
            stage(2 * e + 1, 2, g)
            wk = taps(1, g)
            wv = taps(2, g)
            for lo in range(0, length, ROWS):
                kk = causal(2 * e, wk, lo, ROWS)
                vv = causal(2 * e + 1, wv, lo, ROWS)
                ks[g, lo : lo + ROWS, :] = kk
                vs[g, lo : lo + ROWS, :] = vv
                pb[g, lo : lo + ROWS, :] = (kk * vv).astype(BF16)
            s = mm(tailf[g, 0 : 2 * MODES], pb[g])
            sy[0, y, p, e] = s[0:MODES] + s[MODES : 2 * MODES]
        y_start(0, p)

    @pl.loop(0, pairs)
    def _(p):
        y_total(0, p)
        for e in range(PAIR):
            g = p * PAIR + e
            stage(e, 0, g)
            w = taps(0, g)
            skip = skipin[pl.ds(g, 1), :]
            for b in range(blocks):
                r = slice(b * GROUP_CH, (b + 1) * GROUP_CH)
                here = mm(wf[g, :, (blocks - 1 - b) * GROUP_CH :], pb[g, 0 : (b + 1) * GROUP_CH, :])
                for lo in range(b * GROUP_CH, (b + 1) * GROUP_CH, ROWS):
                    qs[g, lo : lo + ROWS, :] = causal(e, w, lo, ROWS)
                fw[g, r, :] = here + skip * pb[g, r, :].astype(F32)

    acc[...] = jnp.zeros_like(acc)
    load(3).wait()

    @pl.loop(0, pairs)
    def _(p):
        z_wait(0, p)
        states_in = [entering(0, p, e) for e in range(PAIR)]
        for b in range(blocks):
            r = slice(b * GROUP_CH, (b + 1) * GROUP_CH)
            squares = acc[0, r, :]
            aligned = acc[1, r, :]
            for e in range(PAIR):
                g = p * PAIR + e
                gain = gainin[pl.ds(g, 1), :]
                f = fw[g, r, :] + mm(af[g], states_in[e][b])
                fw[g, r, :] = f
                gated = qs[g, r, :] * f
                squares = squares + gated * gated
                aligned = aligned + (xin[3, r, cols(g)].astype(F32) * gain) * gated
            acc[0, r, :] = squares
            acc[1, r, :] = aligned

    sums = []
    for a in range(2):
        for lo in range(0, length, GROUP_CH):
            sums.append(jnp.sum(acc[a, lo : lo + GROUP_CH, :].T, axis=0, keepdims=True))
    cs[tp] = jnp.concatenate(sums, axis=0)

    def sums_copy(step):
        return pltpu.make_async_remote_copy(
            src_ref=cs.at[tp],
            dst_ref=cs.at[tp],
            send_sem=csend.at[step],
            recv_sem=crecv.at[tp],
            device_id=(me, lax.rem(tp + step, ntp)),
            device_id_type=MESH,
        )

    for step in range(1, ntp):
        sums_copy(step).start()
    for step in range(1, ntp):
        slot = lax.rem(tp + step, ntp)
        pltpu.make_async_copy(cs.at[slot], cs.at[slot], crecv.at[slot]).wait()
    total = cs[0]
    for i in range(1, ntp):
        total = total + cs[i]
    width = float(groups * GROUP_CH * ntp)
    scale = lax.rsqrt(total[0:blocks] / width + EPSILON)
    cubed = scale * scale * scale * (total[blocks : 2 * blocks] / width)
    for b in range(blocks):
        r = slice(b * GROUP_CH, (b + 1) * GROUP_CH)
        scales[0, r, :] = jnp.broadcast_to(scale[b : b + 1, :], (GROUP_CH, GROUP_CH)).T
        scales[1, r, :] = jnp.broadcast_to(cubed[b : b + 1, :], (GROUP_CH, GROUP_CH)).T

    def edge_copy(a, g):
        return pltpu.make_async_remote_copy(
            src_ref=(dq, dk, dv)[a].at[g, pl.ds(0, 8), :],
            dst_ref=edge.at[a, g],
            send_sem=gsend.at[a, g],
            recv_sem=grecv.at[a, g],
            device_id=(behind, tp),
            device_id_type=MESH,
        )

    @pl.loop(0, pairs)
    def _(p):
        for e in range(PAIR):
            g = p * PAIR + e
            gain = gainin[pl.ds(g, 1), :]
            for lo in range(0, length, ROWS):
                r = slice(lo, lo + ROWS)
                q = qs[g, r, :]
                f = fw[g, r, :]
                gated = q * f
                scale = scales[0, r, :]
                mixed[r, cols(g)] = (gated * scale * gain).astype(BF16)
                d_gated = scale * (xin[3, r, cols(g)].astype(F32) * gain) - scales[1, r, :] * gated
                dq[g, r, :] = d_gated * f
                pb[g, r, :] = (d_gated * q).astype(BF16)
            s = mm(tailb[g, 0 : 2 * MODES], pb[g])
            sy[1, y, p, e] = s[0:MODES] + s[MODES : 2 * MODES]
        y_start(1, p)
        for e in range(PAIR):
            edge_copy(0, p * PAIR + e).start()

    def attach(a, g):
        edge_copy(a, g).wait_recv()
        (dq, dk, dv)[a][g, length : length + 8, :] = edge[a, g] * final

    @pl.loop(0, pairs)
    def _(p):
        y_total(1, p)
        for e in range(PAIR):
            attach(0, p * PAIR + e)
        for e in range(PAIR):
            g = p * PAIR + e
            w = taps(0, g)
            skip = skipin[pl.ds(g, 1), :]
            for b in range(blocks):
                r = slice(b * GROUP_CH, (b + 1) * GROUP_CH)
                here = mm(wb[g, :, 0 : (blocks - b) * GROUP_CH], pb[g, b * GROUP_CH :, :])
                for lo in range(b * GROUP_CH, (b + 1) * GROUP_CH, ROWS):
                    gq[lo : lo + ROWS, cols(g)] = later(dq, g, w, lo, ROWS).astype(BF16)
                fw[g, r, :] = here + skip * pb[g, r, :].astype(F32)

    @pl.loop(0, pairs)
    def _(p):
        z_wait(1, p)
        states_in = [entering(1, p, e) for e in range(PAIR)]
        for e in range(PAIR):
            g = p * PAIR + e
            for b in range(blocks):
                r = slice(b * GROUP_CH, (b + 1) * GROUP_CH)
                dp = fw[g, r, :] + mm(ab[g], states_in[e][b])
                dk[g, r, :] = dp * vs[g, r, :]
                dv[g, r, :] = dp * ks[g, r, :]
        for e in range(PAIR):
            edge_copy(1, p * PAIR + e).start()
            edge_copy(2, p * PAIR + e).start()

    @pl.loop(0, pairs)
    def _(p):
        for e in range(PAIR):
            attach(1, p * PAIR + e)
        for e in range(PAIR):
            g = p * PAIR + e
            w = taps(1, g)
            for lo in range(0, length, ROWS):
                gk[lo : lo + ROWS, cols(g)] = later(dk, g, w, lo, ROWS).astype(BF16)

    for a in range(3):
        halo_copy(a).wait_send()
    for step in range(1, ntp):
        sums_copy(step).wait_send()

    @pl.loop(0, pairs)
    def _(p):
        for d in range(2):
            for step in range(1, NY):
                state_copy(sy, ysend, yrecv, y, d, p, step, ypeer(step)).wait_send()
            for step in range(1, NZ):
                state_copy(sz, zsend, zrecv, z, d, p, step, zpeer(step)).wait_send()
        for e in range(PAIR):
            for a in range(3):
                edge_copy(a, p * PAIR + e).wait_send()
            attach(2, p * PAIR + e)


def tail_kernel(mixed, gq, gk, dv, w_hbm, mixed_hbm, gq_hbm, gk_hbm, gv_hbm, win, out, sem, out_sem):
    groups, length = dv.shape[0], out.shape[1]
    taps_in = pltpu.make_async_copy(w_hbm.at[2], win, sem.at[0])
    taps_in.start()
    whole = [
        pltpu.make_async_copy(src, dst, sem.at[1 + i])
        for i, (src, dst) in enumerate(((mixed, mixed_hbm), (gq, gq_hbm), (gk, gk_hbm)))
    ]
    for copy in whole:
        copy.start()
    taps_in.wait()

    def store(g):
        return pltpu.make_async_copy(out.at[g], gv_hbm.at[:, cols(g)], out_sem.at[g])

    @pl.loop(0, groups)
    def _(g):
        w = [win[j : j + 1, cols(g)] for j in range(KER)]
        for lo in range(0, length, ROWS):
            out[g, lo : lo + ROWS, :] = later(dv, g, w, lo, ROWS).astype(BF16)
        store(g).start()

    for copy in whole:
        copy.wait()

    @pl.loop(0, groups)
    def _(g):
        store(g).wait()


def body(q_in, k_in, v_in, short_weight, decay_rate, residue, skip, gain, d_out):
    length, channels = q_in.shape
    groups = channels // GROUP_CH
    pairs = groups // PAIR
    ntp = lax.axis_size("tp")
    states = groups * MODES
    blocks = length // GROUP_CH
    vmem = pltpu.VMEM
    dma = pltpu.SemaphoreType.DMA
    here = pl.BlockSpec(memory_space=pltpu.VMEM)
    anywhere = pl.BlockSpec(memory_space=pl.ANY)
    scratch = [
        vmem((4, length, channels), BF16),
        vmem(short_weight.shape, F32),
        vmem((groups, MODES), F32),
        vmem((groups, MODES), F32),
        vmem((groups, GROUP_CH), F32),
        vmem((groups, GROUP_CH), F32),
        vmem((3, 8, channels), BF16),
        vmem((4, length + 8, GROUP_CH), F32),
        vmem((groups, length, GROUP_CH), F32),
        vmem((groups, length, GROUP_CH), F32),
        vmem((groups, length, GROUP_CH), F32),
        vmem((groups, length, GROUP_CH), BF16),
        vmem((groups, length, GROUP_CH), F32),
        vmem((groups, length + 8, GROUP_CH), F32),
        vmem((groups, length + 8, GROUP_CH), F32),
        vmem((3, groups, 8, GROUP_CH), F32),
        vmem((groups, GROUP_CH, length), BF16),
        vmem((groups, GROUP_CH, length), BF16),
        vmem((groups, GROUP_CH, 3 * MODES), BF16),
        vmem((groups, GROUP_CH, 3 * MODES), BF16),
        vmem((groups, 3 * MODES, length), BF16),
        vmem((groups, 3 * MODES, length), BF16),
        vmem((states, GROUP_CH), F32),
        vmem((groups, 3 * MODES), F32),
        vmem((groups, 3 * MODES), F32),
        vmem((blocks, states, GROUP_CH), F32),
        vmem((3, states, GROUP_CH), F32),
        vmem((2, length, GROUP_CH), F32),
        vmem((2, length, GROUP_CH), F32),
        vmem((pairs, PAIR, MODES, GROUP_CH), F32),
        vmem((2, NY, pairs, PAIR, MODES, GROUP_CH), F32),
        vmem((2, NZ, pairs, PAIR, MODES, GROUP_CH), F32),
        vmem((ntp, 8, GROUP_CH), F32),
        dma((4,)),
        dma((5,)),
        dma((3,)),
        dma((3,)),
        dma((2, NY, pairs)),
        dma((2, NY, pairs)),
        dma((2, NZ, pairs)),
        dma((2, NZ, pairs)),
        dma((ntp,)),
        dma((ntp,)),
        dma((3, groups)),
        dma((3, groups)),
    ]
    mixed, gq, gk, dv = pl.pallas_call(
        functools.partial(main_kernel, ntp),
        out_shape=(
            vmem((length, channels), BF16),
            vmem((length, channels), BF16),
            vmem((length, channels), BF16),
            vmem((groups, length + 8, GROUP_CH), F32),
        ),
        in_specs=[anywhere] * 9,
        out_specs=(here,) * 4,
        scratch_shapes=scratch,
        compiler_params=pltpu.CompilerParams(
            collective_id=0, has_side_effects=True, vmem_limit_bytes=GRANT
        ),
        name="hyena_main",
    )(
        q_in, k_in, v_in, d_out, short_weight, decay_rate, residue,
        skip.reshape(groups, GROUP_CH), gain.reshape(groups, GROUP_CH),
    )
    result = jax.ShapeDtypeStruct((length, channels), BF16)
    return pl.pallas_call(
        tail_kernel,
        out_shape=(result,) * 4,
        in_specs=[here] * 4 + [anywhere],
        out_specs=(anywhere,) * 4,
        scratch_shapes=[
            vmem(short_weight.shape[1:], F32),
            vmem((groups, length, GROUP_CH), BF16),
            dma((4,)),
            dma((groups,)),
        ],
        compiler_params=pltpu.CompilerParams(vmem_limit_bytes=8 * 1024 * 1024),
        name="hyena_tail",
    )(mixed, gq, gk, dv, short_weight)


def solution(mesh):
    in_specs = (
        P("ctx", "tp"),
        P("ctx", "tp"),
        P("ctx", "tp"),
        P(None, None, "tp"),
        P("tp", None),
        P("tp", None),
        P("tp"),
        P("tp"),
        P("ctx", "tp"),
    )
    out_specs = (P("ctx", "tp"), P("ctx", "tp"), P("ctx", "tp"), P("ctx", "tp"))
    return jax.shard_map(body, mesh=mesh, in_specs=in_specs, out_specs=out_specs, check_vma=False)
```

```python
import functools

import jax
import jax.numpy as jnp
from jax import lax
from jax.experimental import pallas as pl
from jax.experimental.pallas import tpu as pltpu
from jax.sharding import PartitionSpec as P

KER = 7
MODES = 16
GROUP_CH = 128
EPSILON = 1e-05
NZ = 4
NY = 4
ROWS = 64
PAIR = 2
GRANT = 61_720_000
MESH = pl.DeviceIdType.MESH
F32 = jnp.float32
BF16 = jnp.bfloat16


def split(x):
    hi = x.astype(BF16)
    lo = (x - hi.astype(F32)).astype(BF16)
    return hi, lo


def mm(a, b):
    return jnp.dot(a, b, preferred_element_type=F32)


def cols(g):
    return pl.ds(pl.multiple_of(g * GROUP_CH, GROUP_CH), GROUP_CH)


def later(src, g, w, lo, rows):
    total = w[0] * src[g, pl.ds(lo, rows), :]
    for j in range(1, KER):
        total = total + w[j] * src[g, pl.ds(lo + j, rows), :]
    return total


def main_kernel(
    ntp,
    q_hbm, k_hbm, v_hbm, d_hbm, w_hbm, rate_hbm, res_hbm, skip_hbm, gain_hbm,
    mixed, gq, gk, dv, wtail,
    xin, win, ratein, resin, skipin, gainin,
    halo, xs, lead, qs, ks, vs, pb, fw, dq, dk, eout, edge, before_k, before_v,
    wf, wb, af, ab, tailf, tailb, hneg, ratew, rate3, coef3, dec, far,
    acc, scales, xpart, sy, sz, cs,
    in_sem, par_sem,
    hsend, hrecv, ysend, yrecv, zsend, zrecv, csend, crecv, gsend, grecv, bsend, brecv,
):
    length = xin.shape[1]
    groups = xin.shape[2] // GROUP_CH
    pairs = groups // PAIR
    states = groups * MODES
    blocks = length // GROUP_CH
    nctx = NZ * NY
    me = lax.axis_index("ctx")
    tp = lax.axis_index("tp")
    z = lax.div(me, NY)
    y = lax.rem(me, NY)
    behind = lax.rem(me + nctx - 1, nctx)
    ahead = lax.rem(me + 1, nctx)

    params = [
        pltpu.make_async_copy(src, dst, par_sem.at[i])
        for i, (src, dst) in enumerate(
            ((rate_hbm, ratein), (res_hbm, resin), (w_hbm, win), (skip_hbm, skipin), (gain_hbm, gainin), (w_hbm.at[2], wtail))
        )
    ]
    for copy in params:
        copy.start()

    def load(a):
        return pltpu.make_async_copy((q_hbm, k_hbm, v_hbm, d_hbm)[a], xin.at[a], in_sem.at[a])

    for a in (1, 2, 0, 3):
        load(a).start()

    bar = pltpu.get_barrier_semaphore()

    def greet(c, t):
        pl.semaphore_signal(bar, inc=1, device_id=(c, t), device_id_type=MESH)

    def ypeer(step):
        return z * NY + lax.rem(y + step, NY)

    def zpeer(step):
        return lax.rem(z + step, NZ) * NY + y

    greet(behind, tp)
    greet(ahead, tp)
    for step in range(1, NY):
        greet(ypeer(step), tp)
    for step in range(1, NZ):
        greet(zpeer(step), tp)
    for step in range(1, ntp):
        greet(me, lax.rem(tp + step, ntp))

    pl.semaphore_wait(bar, 2 + NY - 1 + NZ - 1 + ntp - 1)

    def halo_copy(a):
        src = (q_hbm, k_hbm, v_hbm)[a]
        return pltpu.make_async_remote_copy(
            src_ref=src.at[pl.ds(length - 8, 8), :],
            dst_ref=halo.at[a],
            send_sem=hsend.at[a],
            recv_sem=hrecv.at[a],
            device_id=(ahead, tp),
            device_id_type=MESH,
        )

    for a in (1, 2, 0):
        halo_copy(a).start()

    for copy in params:
        copy.wait()

    rate = ratein[...]
    r2 = rate * rate
    sinhc = 1.0 + r2 * (1 / 6) * (1.0 + r2 * (1 / 20) * (1.0 + r2 * (1 / 42) * (1.0 + r2 * (1 / 72) * (1.0 + r2 * (1 / 110)))))
    coef = resin[...] * jnp.sqrt(2.0 * rate * jnp.exp(-rate) * sinhc)
    rate3[...] = jnp.concatenate([rate] * 3, axis=1)
    coef3[...] = jnp.concatenate([coef] * 3, axis=1)
    row_i = lax.broadcasted_iota(jnp.int32, (MODES, MODES), 0)
    col_i = lax.broadcasted_iota(jnp.int32, (MODES, MODES), 1)
    yf = y.astype(F32)
    for g in range(groups):
        m = slice(g * MODES, (g + 1) * MODES)
        column = jnp.sum(
            jnp.where(row_i == col_i, jnp.broadcast_to(rate[g : g + 1, :], (MODES, MODES)), 0.0), axis=1, keepdims=True
        )
        wide = jnp.broadcast_to(column, (MODES, GROUP_CH))
        ratew[m, :] = wide
        for i in range(blocks):
            dec[i, m, :] = jnp.exp(wide * (-1.0 * GROUP_CH * (i + 1)))
        far[0, m, :] = jnp.exp(wide * (-float(length) * yf))
        far[1, m, :] = jnp.exp(wide * (-float(length) * (NY - 1.0 - yf)))
        far[2, m, :] = jnp.exp(wide * (-float(length) * NY))

    i_idx = lax.broadcasted_iota(jnp.int32, (GROUP_CH, 3 * MODES), 0).astype(F32)
    first = lax.broadcasted_iota(jnp.int32, (GROUP_CH, 3 * MODES), 1) < 2 * MODES
    lag = lax.broadcasted_iota(jnp.int32, (MODES, GROUP_CH), 1).astype(F32)
    ti = lax.broadcasted_iota(jnp.int32, (GROUP_CH, GROUP_CH), 0)
    tj = lax.broadcasted_iota(jnp.int32, (GROUP_CH, GROUP_CH), 1)

    def tables(d):
        grow, tail, table = ((af, tailf, wf), (ab, tailb, wb))[d]

        @pl.loop(0, pairs)
        def _(p):
            for e in range(PAIR):
                g = p * PAIR + e
                x = coef3[pl.ds(g, 1), :] * jnp.exp(rate3[pl.ds(g, 1), :] * (i_idx if d else float(GROUP_CH - 1) - i_idx))
                hi = x.astype(BF16).astype(F32)
                grow[g] = jnp.where(first, hi, x - hi).astype(BF16)
                wide = ratew[pl.ds(pl.multiple_of(g * MODES, MODES), MODES), :]
                for b in range(blocks):
                    at = lag + float(b * GROUP_CH)
                    c = slice(b * GROUP_CH, (b + 1) * GROUP_CH)
                    hi, lo = split(jnp.exp(-wide * (at if d else float(length - 1) - at)))
                    tail[g, 0:MODES, c] = hi
                    tail[g, MODES : 2 * MODES, c] = lo
                    tail[g, 2 * MODES : 3 * MODES, c] = hi
            for e in range(PAIR):
                g = p * PAIR + e
                for b in range(blocks):
                    c = slice(b * GROUP_CH, (b + 1) * GROUP_CH)
                    w = mm(grow[g], tail[g, :, c])
                    if d == 1 and b == 0:
                        hneg[g] = jnp.where(ti[0:8, 0:8] > tj[0:8, 0:8], w[0:8, 0:8], 0.0).astype(BF16)
                        w = jnp.where(tj >= ti, w, 0.0)
                    if d == 0 and b == blocks - 1:
                        w = jnp.where(ti >= tj, w, 0.0)
                    table[g, :, c] = w.astype(BF16)

    tables(0)

    inner = (me > 0).astype(F32)
    final = (me < nctx - 1).astype(F32)

    def taps(a, g):
        return [win[a, j : j + 1, cols(g)] for j in range(KER)]

    def stage(slot, a, g):
        xs[slot, 0:8, :] = halo[a, :, cols(g)].astype(F32) * inner
        for lo in range(0, length, ROWS):
            xs[slot, 8 + lo : 8 + lo + ROWS, :] = xin[a, lo : lo + ROWS, cols(g)].astype(F32)

    def causal(slot, w, lo, rows):
        total = w[0] * xs[slot, pl.ds(8 + lo, rows), :]
        for j in range(1, KER):
            total = total + w[j] * xs[slot, pl.ds(8 + lo - j, rows), :]
        return total

    def state_copy(buf, send, recv, mine, d, p, step, peer):
        return pltpu.make_async_remote_copy(
            src_ref=buf.at[d, mine, p],
            dst_ref=buf.at[d, mine, p],
            send_sem=send.at[d, step, p],
            recv_sem=recv.at[d, mine, p],
            device_id=(peer, tp),
            device_id_type=MESH,
        )

    def y_start(d, p):
        for step in (1, 3, 2):
            state_copy(sy, ysend, yrecv, y, d, p, step, ypeer(step)).start()

    def z_start(d, p):
        for step in (1, 3, 2):
            state_copy(sz, zsend, zrecv, z, d, p, step, zpeer(step)).start()

    def arrived(buf, recv, d, p, slot):
        pltpu.make_async_copy(buf.at[d, slot, p], buf.at[d, slot, p], recv.at[d, slot, p]).wait()

    def modes(g):
        return pl.ds(pl.multiple_of(g * MODES, MODES), MODES)

    def y_total(d, p):
        for step in (1, 3, 2):
            arrived(sy, yrecv, d, p, lax.rem(y + step, NY))
        for e in range(PAIR):
            g = p * PAIR + e
            decay = dec[blocks - 1, modes(g), :]
            part = jnp.zeros((MODES, GROUP_CH), F32)
            total = jnp.zeros((MODES, GROUP_CH), F32)
            for i in range(NY) if d == 0 else reversed(range(NY)):
                s = sy[d, i, p, e]
                before = (i < y) if d == 0 else (i > y)
                part = jnp.where(before, decay * part + s, part)
                total = decay * total + s
            xpart[p, e] = part
            sz[d, z, p, e] = total
        z_start(d, p)

    def z_wait(d, p):
        for step in (1, 3, 2):
            arrived(sz, zrecv, d, p, lax.rem(z + step, NZ))

    def entering(d, p, e):
        m = modes(p * PAIR + e)
        decay = far[2, m, :]
        total = jnp.zeros((MODES, GROUP_CH), F32)
        for i in range(NZ) if d == 0 else reversed(range(NZ)):
            before = (i < z) if d == 0 else (i > z)
            total = jnp.where(before, decay * total + sz[d, i, p, e], total)
        x = xpart[p, e] + far[d, m, :] * total
        parts = []
        if d == 1:
            hi, lo = split(x)
            parts.append(jnp.concatenate([hi, lo, hi], axis=0))
        for b in range(blocks):
            hi, lo = split(x * dec[b if d == 0 else blocks - 1 - b, m, :])
            parts.append(jnp.concatenate([hi, lo, hi], axis=0))
        return parts

    def lead_rows(a, g, w):
        total = w[0] * lead[a, g, 8:16, :]
        for j in range(1, KER):
            total = total + w[j] * lead[a, g, 8 - j : 16 - j, :]
        return total

    for a in (1, 2):
        load(a).wait()

    @pl.loop(0, pairs)
    def _(p):
        for e in range(PAIR):
            g = p * PAIR + e
            for a in (1, 2):
                for lo in range(0, length, ROWS):
                    xs[2 * e + a - 1, 8 + lo : 8 + lo + ROWS, :] = xin[a, lo : lo + ROWS, cols(g)].astype(F32)
                lead[a, g, 8:16, :] = xin[a, 0:8, cols(g)].astype(F32)
            wk = taps(1, g)
            wv = taps(2, g)
            for lo in range(0, length, ROWS):
                skipped = 8 if lo == 0 else 0
                r = slice(lo + skipped, lo + ROWS)
                kk = causal(2 * e, wk, lo + skipped, ROWS - skipped)
                vv = causal(2 * e + 1, wv, lo + skipped, ROWS - skipped)
                ks[g, r, :] = kk
                vs[g, r, :] = vv
                pb[g, r, :] = (kk * vv).astype(BF16)

    for a in (1, 2):
        halo_copy(a).wait_recv()
    for g in range(groups):
        for a in (1, 2):
            lead[a, g, 0:8, :] = halo[a, :, cols(g)].astype(F32) * inner
        kk = lead_rows(1, g, taps(1, g))
        vv = lead_rows(2, g, taps(2, g))
        ks[g, 0:8, :] = kk
        vs[g, 0:8, :] = vv
        pb[g, 0:8, :] = (kk * vv).astype(BF16)
    for g in range(groups):
        s = mm(tailf[g, 0 : 2 * MODES], pb[g])
        sy[0, y, g // PAIR, g % PAIR] = s[0:MODES] + s[MODES : 2 * MODES]
    for p in range(pairs):
        y_start(0, p)

    def before_copy(a):
        return pltpu.make_async_remote_copy(
            src_ref=(ks, vs)[a].at[:, pl.ds(0, 8), :],
            dst_ref=(before_k, before_v)[a],
            send_sem=bsend.at[a],
            recv_sem=brecv.at[a],
            device_id=(behind, tp),
            device_id_type=MESH,
        )

    for a in range(2):
        before_copy(a).start()

    load(0).wait()
    halo_copy(0).wait_recv()

    @pl.loop(0, pairs)
    def _(p):
        for e in range(PAIR):
            g = p * PAIR + e
            stage(e, 0, g)
            w = taps(0, g)
            for lo in range(0, length, ROWS):
                qs[g, lo : lo + ROWS, :] = causal(e, w, lo, ROWS)

    tables(1)

    @pl.loop(0, pairs)
    def _(p):
        y_total(0, p)
        for e in range(PAIR):
            g = p * PAIR + e
            skip = skipin[pl.ds(g, 1), :]
            for b in range(blocks):
                r = slice(b * GROUP_CH, (b + 1) * GROUP_CH)
                here = mm(wf[g, :, (blocks - 1 - b) * GROUP_CH :], pb[g, 0 : (b + 1) * GROUP_CH, :])
                fw[g, r, :] = here + skip * pb[g, r, :].astype(F32)

    acc[...] = jnp.zeros_like(acc)
    load(3).wait()

    @pl.loop(0, pairs)
    def _(p):
        z_wait(0, p)
        states_in = [entering(0, p, e) for e in range(PAIR)]
        for b in range(blocks):
            r = slice(b * GROUP_CH, (b + 1) * GROUP_CH)
            squares = acc[0, r, :]
            aligned = acc[1, r, :]
            for e in range(PAIR):
                g = p * PAIR + e
                gain = gainin[pl.ds(g, 1), :]
                f = fw[g, r, :] + mm(af[g], states_in[e][b])
                fw[g, r, :] = f
                gated = qs[g, r, :] * f
                squares = squares + gated * gated
                aligned = aligned + (xin[3, r, cols(g)].astype(F32) * gain) * gated
            acc[0, r, :] = squares
            acc[1, r, :] = aligned

    sums = []
    for a in range(2):
        for lo in range(0, length, GROUP_CH):
            sums.append(jnp.sum(acc[a, lo : lo + GROUP_CH, :].T, axis=0, keepdims=True))
    cs[tp] = jnp.concatenate(sums, axis=0)

    def sums_copy(step):
        return pltpu.make_async_remote_copy(
            src_ref=cs.at[tp],
            dst_ref=cs.at[tp],
            send_sem=csend.at[step],
            recv_sem=crecv.at[tp],
            device_id=(me, lax.rem(tp + step, ntp)),
            device_id_type=MESH,
        )

    for step in range(1, ntp):
        sums_copy(step).start()
    for step in range(1, ntp):
        slot = lax.rem(tp + step, ntp)
        pltpu.make_async_copy(cs.at[slot], cs.at[slot], crecv.at[slot]).wait()
    total = cs[0]
    for i in range(1, ntp):
        total = total + cs[i]
    width = float(groups * GROUP_CH * ntp)
    scale = lax.rsqrt(total[0:blocks] / width + EPSILON)
    cubed = scale * scale * scale * (total[blocks : 2 * blocks] / width)
    for b in range(blocks):
        r = slice(b * GROUP_CH, (b + 1) * GROUP_CH)
        scales[0, r, :] = jnp.broadcast_to(scale[b : b + 1, :], (GROUP_CH, GROUP_CH)).T
        scales[1, r, :] = jnp.broadcast_to(cubed[b : b + 1, :], (GROUP_CH, GROUP_CH)).T

    def edge_copy(p):
        return pltpu.make_async_remote_copy(
            src_ref=eout.at[p],
            dst_ref=edge.at[p],
            send_sem=gsend.at[p],
            recv_sem=grecv.at[p],
            device_id=(behind, tp),
            device_id_type=MESH,
        )

    @pl.loop(0, pairs)
    def _(p):
        for e in range(PAIR):
            g = p * PAIR + e
            gain = gainin[pl.ds(g, 1), :]
            for lo in range(0, length, ROWS):
                r = slice(lo, lo + ROWS)
                q = qs[g, r, :]
                f = fw[g, r, :]
                d_gated = scales[0, r, :] * (xin[3, r, cols(g)].astype(F32) * gain) - scales[1, r, :] * (q * f)
                dq[g, r, :] = d_gated
                d_filtered = (d_gated * q).astype(BF16)
                pb[g, r, :] = d_filtered
                if lo == 0:
                    eout[p, 0, e] = d_gated[0:8] * f[0:8]
                    eout[p, 1, e] = d_filtered[0:8].astype(F32)
            s = mm(tailb[g, 0 : 2 * MODES], pb[g])
            sy[1, y, p, e] = s[0:MODES] + s[MODES : 2 * MODES]
        y_start(1, p)
        edge_copy(p).start()

    @pl.loop(0, pairs)
    def _(p):
        for e in range(PAIR):
            g = p * PAIR + e
            gain = gainin[pl.ds(g, 1), :]
            for lo in range(0, length, ROWS):
                r = slice(lo, lo + ROWS)
                f = fw[g, r, :]
                mixed[r, cols(g)] = (qs[g, r, :] * f * scales[0, r, :] * gain).astype(BF16)
                dq[g, r, :] = dq[g, r, :] * f

    @pl.loop(0, pairs)
    def _(p):
        y_total(1, p)
        for e in range(PAIR):
            g = p * PAIR + e
            skip = skipin[pl.ds(g, 1), :]
            for b in range(blocks):
                r = slice(b * GROUP_CH, (b + 1) * GROUP_CH)
                here = mm(wb[g, :, 0 : (blocks - b) * GROUP_CH], pb[g, b * GROUP_CH :, :])
                fw[g, r, :] = here + skip * pb[g, r, :].astype(F32)

    @pl.loop(0, pairs)
    def _(p):
        edge_copy(p).wait_recv()
        for e in range(PAIR):
            g = p * PAIR + e
            dq[g, length : length + 8, :] = edge[p, 0, e] * final
            w = taps(0, g)
            for lo in range(0, length, ROWS):
                gq[lo : lo + ROWS, cols(g)] = later(dq, g, w, lo, ROWS).astype(BF16)

    for a in range(2):
        before_copy(a).wait_recv()

    @pl.loop(0, pairs)
    def _(p):
        z_wait(1, p)
        states_in = [entering(1, p, e) for e in range(PAIR)]
        for e in range(PAIR):
            g = p * PAIR + e
            past = edge[p, 1, e]
            dp = (
                mm(ab[g, 0:8, :], states_in[e][0])
                - mm(hneg[g], past.astype(BF16))
                + skipin[pl.ds(g, 1), :] * past
            ) * final
            dk[g, length : length + 8, :] = dp * before_v[g]
            dv[g, length : length + 8, :] = dp * before_k[g]
            for b in range(blocks):
                r = slice(b * GROUP_CH, (b + 1) * GROUP_CH)
                dp = fw[g, r, :] + mm(ab[g], states_in[e][b + 1])
                dk[g, r, :] = dp * vs[g, r, :]
                dv[g, r, :] = dp * ks[g, r, :]

    @pl.loop(0, pairs)
    def _(p):
        for e in range(PAIR):
            g = p * PAIR + e
            w = taps(1, g)
            for lo in range(0, length, ROWS):
                gk[lo : lo + ROWS, cols(g)] = later(dk, g, w, lo, ROWS).astype(BF16)

    for a in range(3):
        halo_copy(a).wait_send()
    for a in range(2):
        before_copy(a).wait_send()
    for step in range(1, ntp):
        sums_copy(step).wait_send()

    @pl.loop(0, pairs)
    def _(p):
        for d in range(2):
            for step in range(1, NY):
                state_copy(sy, ysend, yrecv, y, d, p, step, ypeer(step)).wait_send()
            for step in range(1, NZ):
                state_copy(sz, zsend, zrecv, z, d, p, step, zpeer(step)).wait_send()
        edge_copy(p).wait_send()


def tail_kernel(mixed, gq, gk, dv, win, mixed_hbm, gq_hbm, gk_hbm, gv_hbm, out, sem, out_sem):
    groups, length = dv.shape[0], out.shape[1]
    whole = [
        pltpu.make_async_copy(src, dst, sem.at[i])
        for i, (src, dst) in enumerate(((mixed, mixed_hbm), (gq, gq_hbm), (gk, gk_hbm)))
    ]
    for copy in whole:
        copy.start()

    def store(g):
        return pltpu.make_async_copy(out.at[g], gv_hbm.at[:, cols(g)], out_sem.at[g])

    @pl.loop(0, groups)
    def _(g):
        w = [win[j : j + 1, cols(g)] for j in range(KER)]
        for lo in range(0, length, ROWS):
            out[g, lo : lo + ROWS, :] = later(dv, g, w, lo, ROWS).astype(BF16)
        store(g).start()

    for copy in whole:
        copy.wait()

    @pl.loop(0, groups)
    def _(g):
        store(g).wait()


def body(q_in, k_in, v_in, short_weight, decay_rate, residue, skip, gain, d_out):
    length, channels = q_in.shape
    groups = channels // GROUP_CH
    pairs = groups // PAIR
    ntp = lax.axis_size("tp")
    states = groups * MODES
    blocks = length // GROUP_CH
    vmem = pltpu.VMEM
    dma = pltpu.SemaphoreType.DMA
    here = pl.BlockSpec(memory_space=pltpu.VMEM)
    anywhere = pl.BlockSpec(memory_space=pl.ANY)
    scratch = [
        vmem((4, length, channels), BF16),
        vmem(short_weight.shape, F32),
        vmem((groups, MODES), F32),
        vmem((groups, MODES), F32),
        vmem((groups, GROUP_CH), F32),
        vmem((groups, GROUP_CH), F32),
        vmem((3, 8, channels), BF16),
        vmem((4, length + 8, GROUP_CH), F32),
        vmem((3, groups, 16, GROUP_CH), F32),
        vmem((groups, length, GROUP_CH), F32),
        vmem((groups, length, GROUP_CH), F32),
        vmem((groups, length, GROUP_CH), F32),
        vmem((groups, length, GROUP_CH), BF16),
        vmem((groups, length, GROUP_CH), F32),
        vmem((groups, length + 8, GROUP_CH), F32),
        vmem((groups, length + 8, GROUP_CH), F32),
        vmem((pairs, 2, PAIR, 8, GROUP_CH), F32),
        vmem((pairs, 2, PAIR, 8, GROUP_CH), F32),
        vmem((groups, 8, GROUP_CH), F32),
        vmem((groups, 8, GROUP_CH), F32),
        vmem((groups, GROUP_CH, length), BF16),
        vmem((groups, GROUP_CH, length), BF16),
        vmem((groups, GROUP_CH, 3 * MODES), BF16),
        vmem((groups, GROUP_CH, 3 * MODES), BF16),
        vmem((groups, 3 * MODES, length), BF16),
        vmem((groups, 3 * MODES, length), BF16),
        vmem((groups, 8, 8), BF16),
        vmem((states, GROUP_CH), F32),
        vmem((groups, 3 * MODES), F32),
        vmem((groups, 3 * MODES), F32),
        vmem((blocks, states, GROUP_CH), F32),
        vmem((3, states, GROUP_CH), F32),
        vmem((2, length, GROUP_CH), F32),
        vmem((2, length, GROUP_CH), F32),
        vmem((pairs, PAIR, MODES, GROUP_CH), F32),
        vmem((2, NY, pairs, PAIR, MODES, GROUP_CH), F32),
        vmem((2, NZ, pairs, PAIR, MODES, GROUP_CH), F32),
        vmem((ntp, 8, GROUP_CH), F32),
        dma((4,)),
        dma((6,)),
        dma((3,)),
        dma((3,)),
        dma((2, NY, pairs)),
        dma((2, NY, pairs)),
        dma((2, NZ, pairs)),
        dma((2, NZ, pairs)),
        dma((ntp,)),
        dma((ntp,)),
        dma((pairs,)),
        dma((pairs,)),
        dma((2,)),
        dma((2,)),
    ]
    mixed, gq, gk, dv, taps = pl.pallas_call(
        functools.partial(main_kernel, ntp),
        out_shape=(
            vmem((length, channels), BF16),
            vmem((length, channels), BF16),
            vmem((length, channels), BF16),
            vmem((groups, length + 8, GROUP_CH), F32),
            vmem(short_weight.shape[1:], F32),
        ),
        in_specs=[anywhere] * 9,
        out_specs=(here,) * 5,
        scratch_shapes=scratch,
        compiler_params=pltpu.CompilerParams(
            collective_id=0, has_side_effects=True, vmem_limit_bytes=GRANT
        ),
        name="hyena_main",
    )(
        q_in, k_in, v_in, d_out, short_weight, decay_rate, residue,
        skip.reshape(groups, GROUP_CH), gain.reshape(groups, GROUP_CH),
    )
    result = jax.ShapeDtypeStruct((length, channels), BF16)
    return pl.pallas_call(
        tail_kernel,
        out_shape=(result,) * 4,
        in_specs=[here] * 5,
        out_specs=(anywhere,) * 4,
        scratch_shapes=[
            vmem((groups, length, GROUP_CH), BF16),
            dma((3,)),
            dma((groups,)),
        ],
        compiler_params=pltpu.CompilerParams(vmem_limit_bytes=8 * 1024 * 1024),
        name="hyena_tail",
    )(mixed, gq, gk, dv, taps)


def solution(mesh):
    in_specs = (
        P("ctx", "tp"),
        P("ctx", "tp"),
        P("ctx", "tp"),
        P(None, None, "tp"),
        P("tp", None),
        P("tp", None),
        P("tp"),
        P("tp"),
        P("ctx", "tp"),
    )
    out_specs = (P("ctx", "tp"), P("ctx", "tp"), P("ctx", "tp"), P("ctx", "tp"))
    return jax.shard_map(body, mesh=mesh, in_specs=in_specs, out_specs=out_specs, check_vma=False)
```
